32 devices in a mesh: pp: 4 (over y, core), cp: 4 (over z), tp: 2 (over x).
Axes of the slice: x: 2, y: 2, z: 4, core: 2. Of those that a mesh axis runs over, the one named last changes fastest.
Arguments:
- queries: bfloat16 [4, 1024, 8192], P('pp', 'cp', 'tp'), may hold values from -150 to 150
- keys: bfloat16 [4, 1024, 1024], P('pp', 'cp', 'tp'), may hold values from -6 to 6
- values: bfloat16 [4, 1024, 1024], P('pp', 'cp', 'tp'), may hold values from -6 to 6
- span_order: int32 [8], replicated, may hold values from 0 to 7, each once
Outputs:
- forwarded: bfloat16 [4, 1024, 8192], P('pp', ('cp', 'tp'))
The draws below stay inside these ranges and needn't reach their ends.
All inputs are finite; a program needn't handle non-finite values.
Results may differ from the reference program's by a relative error of at most 0.005.
Values may be sent and summed in bfloat16 or wider, within the bound.
A program may use at most 64 MiB of HBM per device.

```python
import jax
import jax.numpy as jnp
from jax import lax

HD = 128
QH = 64
KVH = 8
TOKENS = 1024
SPAN = 128
NCHUNK = 8
SECTIONS = 4


def base_keys(key):
    raw = jax.random.normal(jax.random.fold_in(key, 11), (SECTIONS, TOKENS, KVH * HD), jnp.float32)
    return jnp.clip(raw, -6.0, 6.0)


def draw_keys(key, part):
    return base_keys(key).astype(jnp.bfloat16)


def draw_queries(key, part):
    raw = jax.random.normal(jax.random.fold_in(key, 23), (SECTIONS, TOKENS, QH * HD), jnp.float32)
    drawn = jnp.clip(2.5 * raw, -15.0, 15.0)
    return drawn.astype(jnp.bfloat16)


def block_scale(rng, shape, cuts, low, largest):
    gain, own = 1.0, jax.random.fold_in(rng, 6)
    for position, parts in cuts:
        draws = jnp.exp(jax.random.uniform(jax.random.fold_in(own, position), (parts,), jnp.float32, low / len(cuts), largest / len(cuts)))
        gain = gain * jnp.repeat(draws, shape[position] // parts).reshape([-1 if axis == position else 1 for axis in range(len(shape))])
    return gain


def scatter_about(rng, extent, deviation, most, split=(), kind=jnp.bfloat16):
    values = jax.random.normal(rng, extent, jnp.float32) * deviation
    if len(split) > 0:
        values = block_scale(rng, extent, split, -0.22, 0.18) * values
    return jnp.clip(values, min=-most, max=most).astype(kind)


def setup_inputs(seed: int = 0) -> dict:
    key_of = jax.random.split(jax.random.key(seed), 5)
    queries = draw_queries(jax.random.fold_in(key_of[4], 71), 0)
    keys = draw_keys(jax.random.fold_in(key_of[4], 71), 0)
    values = scatter_about(key_of[2], (SECTIONS, TOKENS, KVH * HD), 1.0, 6.0, ((0, 4), (1, 4), (2, 2)))
    span_order = jax.random.permutation(key_of[3], NCHUNK).astype(jnp.int32)
    return {"queries": queries, "keys": keys, "values": values, "span_order": span_order}


def row_positions(span_order):
    rows = jnp.arange(TOKENS, dtype=jnp.int32)
    return span_order[rows // SPAN].astype(jnp.int32) * SPAN + rows % SPAN


def one_section(section_data, positions):
    queries, keys, values = section_data
    group = QH // KVH
    visible = positions[None, :] <= positions[:, None]
    scale = 1.0 / (HD ** 0.5)

    def one_head(head):
        kv_head = head // group
        query_rows = lax.dynamic_slice_in_dim(queries, head * HD, HD, 1)
        key_rows = lax.dynamic_slice_in_dim(keys, kv_head * HD, HD, 1)
        value_rows = lax.dynamic_slice_in_dim(values, kv_head * HD, HD, 1)
        score = jnp.dot(query_rows, key_rows.T, preferred_element_type=jnp.float32) * scale
        score = jnp.where(visible, score, jnp.float32(-1e30))
        top = jnp.max(score, axis=1, keepdims=True)
        weight = jnp.where(visible, jnp.exp(score - top), jnp.float32(0.0))
        total = jnp.sum(weight, axis=1, keepdims=True)
        mixed = jnp.dot(weight.astype(jnp.bfloat16), value_rows, preferred_element_type=jnp.float32)
        return (mixed / total).astype(jnp.bfloat16)

    heads_out = lax.map(one_head, jnp.arange(QH, dtype=jnp.int32))
    return jnp.transpose(heads_out, (1, 0, 2)).reshape(TOKENS, QH * HD)


def reference(queries, keys, values, span_order):
    positions = row_positions(span_order)
    attended = lax.map(lambda data: one_section(data, positions), (queries, keys, values))
    return jnp.roll(attended, 1, axis=0)
```

```python
import functools
import math

import jax
import jax.numpy as jnp
from jax import lax
from jax.experimental import pallas as pl
from jax.experimental.pallas import tpu as pltpu
from jax.sharding import PartitionSpec as P

HD = 128
SPAN = 128
MESH = pl.DeviceIdType.MESH


def kernel(
    n, tps, pps, kv_heads, group, pieces,
    order_ref, q_ref, k_ref, v_ref, out_ref,
    qbuf, kvbuf, obuf, bias,
    qsem, lsem, right_send, right_recv, left_send, left_recv, out_send, out_recv,
):
    rows = q_ref.shape[0]
    me = lax.axis_index("cp")
    my_tp = lax.axis_index("tp")
    my_pp = lax.axis_index("pp")
    next_pp = lax.rem(my_pp + 1, pps)
    last_pp = lax.rem(my_pp + pps - 1, pps)
    part = rows // tps
    width = group * HD
    per_piece = group // pieces
    piece_width = per_piece * HD

    own = []
    for h in range(kv_heads):
        for which, ref in enumerate((k_ref, v_ref)):
            copy = pltpu.make_async_copy(
                ref.at[:, pl.ds(h * HD, HD)], kvbuf.at[h, me, which], lsem.at[h, which]
            )
            copy.start()
            own.append(copy)
    q_copies = []
    for h in range(kv_heads):
        copy = pltpu.make_async_copy(
            q_ref.at[:, pl.ds(h * width, width)], qbuf.at[:, pl.ds(h * width, width)], qsem.at[h]
        )
        copy.start()
        q_copies.append(copy)

    barrier = pltpu.get_barrier_semaphore()

    @pl.when(me > 0)
    def _():
        pl.semaphore_signal(barrier, inc=1, device_id={"cp": me - 1}, device_id_type=MESH)

    @pl.when(me < n - 1)
    def _():
        pl.semaphore_signal(barrier, inc=1, device_id={"cp": me + 1}, device_id_type=MESH)

    for t in range(tps):
        for other in (next_pp, last_pp):
            pl.semaphore_signal(
                barrier, inc=1, device_id={"pp": other, "tp": t}, device_id_type=MESH
            )
    near = jnp.where(me > 0, 1, 0) + jnp.where(me < n - 1, 1, 0)
    pl.semaphore_wait(barrier, 2 * tps + near)

    def to_right(h, k):
        slot = me - k
        return pltpu.make_async_remote_copy(
            src_ref=kvbuf.at[h, slot], dst_ref=kvbuf.at[h, slot],
            send_sem=right_send.at[h, k], recv_sem=right_recv.at[h, k],
            device_id={"cp": me + 1}, device_id_type=MESH,
        )

    def to_left(h, k):
        slot = me + k
        return pltpu.make_async_remote_copy(
            src_ref=kvbuf.at[h, slot], dst_ref=kvbuf.at[h, slot],
            send_sem=left_send.at[h, k], recv_sem=left_recv.at[h, k],
            device_id={"cp": me - 1}, device_id_type=MESH,
        )

    def from_left(h, k):
        return pltpu.make_async_remote_copy(
            src_ref=kvbuf.at[h, me - k], dst_ref=kvbuf.at[h, me - k],
            send_sem=right_send.at[h, k - 1], recv_sem=right_recv.at[h, k - 1],
            device_id={"cp": me - 1}, device_id_type=MESH,
        )

    def from_right(h, k):
        return pltpu.make_async_remote_copy(
            src_ref=kvbuf.at[h, me + k], dst_ref=kvbuf.at[h, me + k],
            send_sem=left_send.at[h, k - 1], recv_sem=left_recv.at[h, k - 1],
            device_id={"cp": me + 1}, device_id_type=MESH,
        )

    def send_own(h):
        own[2 * h].wait()
        own[2 * h + 1].wait()

        @pl.when(me < n - 1)
        def _():
            to_right(h, 0).start()

        @pl.when(me > 0)
        def _():
            to_left(h, 0).start()

    def take(h, k):
        @pl.when(me - k >= 0)
        def _():
            from_left(h, k).wait_recv()

            @pl.when(me < n - 1)
            def _():
                to_right(h, k).start()

        @pl.when(me + k <= n - 1)
        def _():
            from_right(h, k).wait_recv()

            @pl.when(me > 0)
            def _():
                to_left(h, k).start()

    def out_copy(h, piece, t):
        first = h * width + piece * piece_width
        index = (h * pieces + piece) * tps
        return pltpu.make_async_remote_copy(
            src_ref=obuf.at[pl.ds(t * part, part), pl.ds(first, piece_width)],
            dst_ref=out_ref.at[:, pl.ds(my_tp * kv_heads * width + first, piece_width)],
            send_sem=out_send.at[index + t], recv_sem=out_recv.at[index + my_tp],
            device_id={"pp": next_pp, "tp": t}, device_id_type=MESH,
        )

    def out_arrival(h, piece, t):
        first = h * width + piece * piece_width
        index = (h * pieces + piece) * tps
        return pltpu.make_async_remote_copy(
            src_ref=obuf.at[pl.ds(0, part), pl.ds(first, piece_width)],
            dst_ref=out_ref.at[:, pl.ds(t * kv_heads * width + first, piece_width)],
            send_sem=out_send.at[index + t], recv_sem=out_recv.at[index + t],
            device_id={"pp": last_pp, "tp": t}, device_id_type=MESH,
        )

    send_own(0)
    if kv_heads > 1:
        send_own(1)

    spans = rows // SPAN
    row_in = lax.broadcasted_iota(jnp.int32, (SPAN, SPAN), 0)
    col_in = lax.broadcasted_iota(jnp.int32, (SPAN, SPAN), 1)
    for i in range(spans):
        query_span = order_ref[me * spans + i]

        def mask_span(j, _):
            gap = (query_span - order_ref[j]) * SPAN
            seen = col_in - row_in <= gap
            bias[j, pl.ds(i * SPAN, SPAN), :] = jnp.where(seen, 0.0, -1e30).astype(jnp.float32)
            return 0

        lax.fori_loop(0, n * spans, mask_span, 0)

    keys_all = n * rows

    def attend(h, piece):
        def one_head(g, _):
            first = pl.multiple_of(h * width + (piece * per_piece + g) * HD, HD)
            query = qbuf[:, pl.ds(first, HD)]
            key = kvbuf[h, :, 0].reshape(keys_all, HD)
            value = kvbuf[h, :, 1].reshape(keys_all, HD)
            score = lax.dot_general(
                query, key, (((1,), (1,)), ((), ())), preferred_element_type=jnp.float32
            )
            mask = jnp.concatenate([bias[j] for j in range(n * spans)], axis=1)
            score = score * (1.0 / HD**0.5) + mask
            top = jnp.max(score, axis=1, keepdims=True)
            weight = jnp.exp(score - top)
            total = jnp.sum(weight, axis=1, keepdims=True)
            mixed = jnp.dot(weight.astype(jnp.bfloat16), value, preferred_element_type=jnp.float32)
            obuf[:, pl.ds(first, HD)] = (mixed / total).astype(jnp.bfloat16)
            return 0

        lax.fori_loop(0, per_piece, one_head, 0)

    for h in range(kv_heads):
        for k in range(1, n):
            if h == 0 or k > 1:
                take(h, k)
            if k == 1 and h + 2 < kv_heads:
                send_own(h + 2)
        q_copies[h].wait()
        for piece in range(pieces):
            attend(h, piece)
            if piece == 0 and h + 1 < kv_heads:
                take(h + 1, 1)
            for t in range(tps):
                out_copy(h, piece, t).start()

    for h in range(kv_heads):
        for k in range(n - 1):
            @pl.when((me - k >= 0) & (me < n - 1))
            def _():
                to_right(h, k).wait_send()

            @pl.when((me + k <= n - 1) & (me > 0))
            def _():
                to_left(h, k).wait_send()

    for h in range(kv_heads):
        for piece in range(pieces):
            for t in range(tps):
                out_copy(h, piece, t).wait_send()
                out_arrival(h, piece, t).wait_recv()


def shards(queries, keys, values, span_order):
    query_rows, key_local, value_local = queries[0], keys[0], values[0]
    rows = query_rows.shape[0]
    kv_heads = key_local.shape[1] // HD
    group = query_rows.shape[1] // HD // kv_heads
    n, tps, pps = lax.axis_size("cp"), lax.axis_size("tp"), lax.axis_size("pp")
    pieces = 2
    copies = kv_heads * pieces * tps
    dma = pltpu.SemaphoreType.DMA
    result = pl.pallas_call(
        functools.partial(kernel, n, tps, pps, kv_heads, group, pieces),
        out_shape=jax.ShapeDtypeStruct((rows // tps, tps * query_rows.shape[1]), jnp.bfloat16),
        in_specs=[
            pl.BlockSpec(memory_space=pltpu.SMEM),
            pl.BlockSpec(memory_space=pl.ANY),
            pl.BlockSpec(memory_space=pl.ANY),
            pl.BlockSpec(memory_space=pl.ANY),
        ],
        out_specs=pl.BlockSpec(memory_space=pl.ANY),
        scratch_shapes=[
            pltpu.VMEM(query_rows.shape, jnp.bfloat16),
            pltpu.VMEM((kv_heads, n, 2, rows, HD), jnp.bfloat16),
            pltpu.VMEM(query_rows.shape, jnp.bfloat16),
            pltpu.VMEM((n * rows // SPAN, rows, SPAN), jnp.float32),
            dma((kv_heads,)),
            dma((kv_heads, 2)),
            dma((kv_heads, n)),
            dma((kv_heads, n)),
            dma((kv_heads, n)),
            dma((kv_heads, n)),
            dma((copies,)),
            dma((copies,)),
        ],
        compiler_params=pltpu.CompilerParams(
            collective_id=0, has_side_effects=True, vmem_limit_bytes=56 * 1024 * 1024
        ),
    )(span_order, query_rows, key_local, value_local)
    return result[None]


def solution(mesh):
    in_specs = (P("pp", "cp", "tp"), P("pp", "cp", "tp"), P("pp", "cp", "tp"), P())
    out_specs = P("pp", ("cp", "tp"), None)
    return jax.shard_map(shards, mesh=mesh, in_specs=in_specs, out_specs=out_specs, check_vma=False)
```

```python
import functools
import math

import jax
import jax.numpy as jnp
from jax import lax
from jax.experimental import pallas as pl
from jax.experimental.pallas import tpu as pltpu
from jax.sharding import PartitionSpec as P

HD = 128
SPAN = 128
LOG_SCALE = math.log2(math.e) / math.sqrt(HD)
MESH = pl.DeviceIdType.MESH


def kernel(
    n, tps, pps, kv_heads, group,
    order_ref, q_ref, k_ref, v_ref, out_ref,
    qbuf, kvbuf, obuf, bias, score_a, score_b, part_mixed, part_top, part_total,
    qsem, lsem, right_send, right_recv, left_send, left_recv, out_send, out_recv,
):
    rows = q_ref.shape[0]
    me = lax.axis_index("cp")
    my_tp = lax.axis_index("tp")
    my_pp = lax.axis_index("pp")
    next_pp = lax.rem(my_pp + 1, pps)
    last_pp = lax.rem(my_pp + pps - 1, pps)
    part = rows // tps
    width = group * HD
    pieces = group // 2
    piece_width = 2 * HD

    own = []
    for h in range(kv_heads):
        for which, ref in enumerate((k_ref, v_ref)):
            copy = pltpu.make_async_copy(
                ref.at[:, pl.ds(h * HD, HD)], kvbuf.at[h, me, which], lsem.at[h, which]
            )
            copy.start()
            own.append(copy)
    q_copies = []
    for h in range(kv_heads):
        copy = pltpu.make_async_copy(
            q_ref.at[:, pl.ds(h * width, width)], qbuf.at[:, pl.ds(h * width, width)], qsem.at[h]
        )
        copy.start()
        q_copies.append(copy)

    barrier = pltpu.get_barrier_semaphore()

    @pl.when(me > 0)
    def _():
        pl.semaphore_signal(barrier, inc=1, device_id={"cp": me - 1}, device_id_type=MESH)

    @pl.when(me < n - 1)
    def _():
        pl.semaphore_signal(barrier, inc=1, device_id={"cp": me + 1}, device_id_type=MESH)

    for t in range(tps):
        for other in (next_pp, last_pp):
            pl.semaphore_signal(
                barrier, inc=1, device_id={"pp": other, "tp": t}, device_id_type=MESH
            )
    near = jnp.where(me > 0, 1, 0) + jnp.where(me < n - 1, 1, 0)
    pl.semaphore_wait(barrier, 2 * tps + near)

    def to_right(h, k):
        slot = me - k
        return pltpu.make_async_remote_copy(
            src_ref=kvbuf.at[h, slot], dst_ref=kvbuf.at[h, slot],
            send_sem=right_send.at[h, k], recv_sem=right_recv.at[h, k],
            device_id={"cp": me + 1}, device_id_type=MESH,
        )

    def to_left(h, k):
        slot = me + k
        return pltpu.make_async_remote_copy(
            src_ref=kvbuf.at[h, slot], dst_ref=kvbuf.at[h, slot],
            send_sem=left_send.at[h, k], recv_sem=left_recv.at[h, k],
            device_id={"cp": me - 1}, device_id_type=MESH,
        )

    def from_left(h, k):
        return pltpu.make_async_remote_copy(
            src_ref=kvbuf.at[h, me - k], dst_ref=kvbuf.at[h, me - k],
            send_sem=right_send.at[h, k - 1], recv_sem=right_recv.at[h, k - 1],
            device_id={"cp": me - 1}, device_id_type=MESH,
        )

    def from_right(h, k):
        return pltpu.make_async_remote_copy(
            src_ref=kvbuf.at[h, me + k], dst_ref=kvbuf.at[h, me + k],
            send_sem=left_send.at[h, k - 1], recv_sem=left_recv.at[h, k - 1],
            device_id={"cp": me + 1}, device_id_type=MESH,
        )

    def send_own(h):
        own[2 * h].wait()
        own[2 * h + 1].wait()

        @pl.when(me < n - 1)
        def _():
            to_right(h, 0).start()

        @pl.when(me > 0)
        def _():
            to_left(h, 0).start()

    def take(h, k):
        @pl.when(me - k >= 0)
        def _():
            from_left(h, k).wait_recv()

            @pl.when(me < n - 1)
            def _():
                to_right(h, k).start()

        @pl.when(me + k <= n - 1)
        def _():
            from_right(h, k).wait_recv()

            @pl.when(me > 0)
            def _():
                to_left(h, k).start()

    def take_far(h):
        take(h, n - 1)

    def out_copy(h, piece, t):
        first = pl.multiple_of(h * width + piece * piece_width, HD)
        index = (h * pieces + piece) * tps
        return pltpu.make_async_remote_copy(
            src_ref=obuf.at[pl.ds(t * part, part), pl.ds(first, piece_width)],
            dst_ref=out_ref.at[:, pl.ds(pl.multiple_of(my_tp * kv_heads * width + first, HD), piece_width)],
            send_sem=out_send.at[index + t], recv_sem=out_recv.at[index + my_tp],
            device_id={"pp": next_pp, "tp": t}, device_id_type=MESH,
        )

    def out_arrival(h, piece, t):
        first = pl.multiple_of(h * width + piece * piece_width, HD)
        index = (h * pieces + piece) * tps
        return pltpu.make_async_remote_copy(
            src_ref=obuf.at[pl.ds(0, part), pl.ds(first, piece_width)],
            dst_ref=out_ref.at[:, pl.ds(t * kv_heads * width + first, piece_width)],
            send_sem=out_send.at[index + t], recv_sem=out_recv.at[index + t],
            device_id={"pp": last_pp, "tp": t}, device_id_type=MESH,
        )

    send_own(0)
    if kv_heads > 1:
        send_own(1)

    spans = rows // SPAN
    row_in = lax.broadcasted_iota(jnp.int32, (SPAN, SPAN), 0)
    col_in = lax.broadcasted_iota(jnp.int32, (SPAN, SPAN), 1)
    for i in range(spans):
        query_span = order_ref[me * spans + i]

        def mask_span(j, _):
            gap = (query_span - order_ref[j]) * SPAN
            seen = col_in - row_in <= gap
            bias[j, pl.ds(i * SPAN, SPAN), :] = jnp.where(seen, 0.0, -1e30).astype(jnp.float32)
            return 0

        lax.fori_loop(0, n * spans, mask_span, 0)

    low = jnp.where(me < n // 2, 0, 1)
    far = jnp.where(me < n // 2, n - 1, 0)
    inner = (me > 0) & (me < n - 1)

    def block(h, slot, count, which):
        return kvbuf[h, pl.ds(slot, count), which].reshape(count * rows, HD)

    def head_columns(h, g):
        return pl.ds(pl.multiple_of(h * width + g * HD, HD), HD)

    def score_of(h, g, slot, count):
        return lax.dot_general(
            qbuf[:, head_columns(h, g)], block(h, slot, count, 0),
            (((1,), (1,)), ((), ())), preferred_element_type=jnp.float32,
        )

    def masked(score, slot, count):
        masks = [bias[slot * spans + j] for j in range(count * spans)]
        return score + jnp.concatenate(masks, axis=1)

    def weigh(h, score, top, slot, count):
        weight = jnp.exp2((score - top) * LOG_SCALE)
        total = jnp.sum(weight, axis=1, keepdims=True)
        mixed = jnp.dot(
            weight.astype(jnp.bfloat16), block(h, slot, count, 1),
            preferred_element_type=jnp.float32,
        )
        return mixed, total

    def finish(h, g, mixed, total):
        obuf[:, head_columns(h, g)] = (mixed / total).astype(jnp.bfloat16)

    def send_piece(h, piece):
        for t in range(tps):
            out_copy(h, piece, t).start()

    def pairs(h, slot, count, done, between):
        score_a[:, : count * rows] = score_of(h, 0, slot, count)

        def pair(i, _):
            score_b[:, : count * rows] = score_of(h, 2 * i + 1, slot, count)
            done(2 * i, masked(score_a[:, : count * rows], slot, count))
            following = jnp.minimum(2 * i + 2, group - 1)
            score_a[:, : count * rows] = score_of(h, following, slot, count)
            done(2 * i + 1, masked(score_b[:, : count * rows], slot, count))
            between(i)
            return 0

        lax.fori_loop(0, group // 2, pair, 0)

    def whole_head(h):
        def done(g, score):
            top = jnp.max(score, axis=1, keepdims=True)
            finish(h, g, *weigh(h, score, top, 0, n))

        def between(i):
            send_piece(h, i)
            for k in range(1, n - 1):
                @pl.when((i == min(k - 1, group // 2 - 1)) & inner)
                def _():
                    take(h + 1, k)

        pairs(h, 0, n, done, between)

    def last_head(h):
        def done(g, score):
            top = jnp.max(score, axis=1, keepdims=True)
            mixed, total = weigh(h, score, top, low, n - 1)
            part_mixed[g] = mixed
            part_top[g] = jnp.broadcast_to(top, (rows, HD))
            part_total[g] = jnp.broadcast_to(total, (rows, HD))

        pairs(h, low, n - 1, done, lambda i: None)
        take_far(h)

        def pair(i, _):
            for g in (2 * i, 2 * i + 1):
                score = masked(score_of(h, g, far, 1), far, 1)
                before = part_top[g]
                top = jnp.maximum(before, jnp.max(score, axis=1, keepdims=True))
                fade = jnp.exp2((before - top) * LOG_SCALE)
                mixed, total = weigh(h, score, top[:, :1], far, 1)
                finish(h, g, part_mixed[g] * fade + mixed, part_total[g] * fade + total)
            send_piece(h, i)
            return 0

        lax.fori_loop(0, group // 2, pair, 0)

    for h in range(kv_heads):
        ends = jnp.logical_not(inner)
        if h == 0:
            ends = me >= 0
        for k in range(1, n - 1):
            @pl.when(ends)
            def _():
                take(h, k)

            if k == 1 and h + 2 < kv_heads:
                send_own(h + 2)
        q_copies[h].wait()
        if h < kv_heads - 1:
            take_far(h)
            whole_head(h)
        else:
            last_head(h)

    for h in range(kv_heads):
        for k in range(n - 1):
            @pl.when((me - k >= 0) & (me < n - 1))
            def _():
                to_right(h, k).wait_send()

            @pl.when((me + k <= n - 1) & (me > 0))
            def _():
                to_left(h, k).wait_send()

    for h in range(kv_heads):
        def drain(piece, _):
            for t in range(tps):
                out_copy(h, piece, t).wait_send()
                out_arrival(h, piece, t).wait_recv()
            return 0

        lax.fori_loop(0, pieces, drain, 0)


def place(x_ref, o_ref):
    o_ref[...] = x_ref[...]


def shards(queries, keys, values, span_order):
    query_rows, key_local, value_local = queries[0], keys[0], values[0]
    rows = query_rows.shape[0]
    kv_heads = key_local.shape[1] // HD
    group = query_rows.shape[1] // HD // kv_heads
    n, tps, pps = lax.axis_size("cp"), lax.axis_size("tp"), lax.axis_size("pp")
    copies = kv_heads * (group // 2) * tps
    dma = pltpu.SemaphoreType.DMA
    result = pl.pallas_call(
        functools.partial(kernel, n, tps, pps, kv_heads, group),
        out_shape=jax.ShapeDtypeStruct((rows // tps, tps * query_rows.shape[1]), jnp.bfloat16),
        in_specs=[
            pl.BlockSpec(memory_space=pltpu.SMEM),
            pl.BlockSpec(memory_space=pl.ANY),
            pl.BlockSpec(memory_space=pl.ANY),
            pl.BlockSpec(memory_space=pl.ANY),
        ],
        out_specs=pl.BlockSpec(memory_space=pl.ANY),
        scratch_shapes=[
            pltpu.VMEM(query_rows.shape, jnp.bfloat16),
            pltpu.VMEM((kv_heads, n, 2, rows, HD), jnp.bfloat16),
            pltpu.VMEM(query_rows.shape, jnp.bfloat16),
            pltpu.VMEM((n * rows // SPAN, rows, SPAN), jnp.float32),
            pltpu.VMEM((rows, n * rows), jnp.float32),
            pltpu.VMEM((rows, n * rows), jnp.float32),
            pltpu.VMEM((group, rows, HD), jnp.float32),
            pltpu.VMEM((group, rows, HD), jnp.float32),
            pltpu.VMEM((group, rows, HD), jnp.float32),
            dma((kv_heads,)),
            dma((kv_heads, 2)),
            dma((kv_heads, n)),
            dma((kv_heads, n)),
            dma((kv_heads, n)),
            dma((kv_heads, n)),
            dma((copies,)),
            dma((copies,)),
        ],
        compiler_params=pltpu.CompilerParams(
            collective_id=0, has_side_effects=True, vmem_limit_bytes=56 * 1024 * 1024
        ),
    )(span_order, query_rows, key_local, value_local)
    columns = result.shape[1] // 8
    spec = pl.BlockSpec((result.shape[0], columns), lambda i: (0, i))
    placed = pl.pallas_call(
        place,
        grid=(8,),
        out_shape=jax.ShapeDtypeStruct(result.shape, result.dtype),
        in_specs=[spec],
        out_specs=spec,
    )(result)
    return placed[None]


def solution(mesh):
    in_specs = (P("pp", "cp", "tp"), P("pp", "cp", "tp"), P("pp", "cp", "tp"), P())
    out_specs = P("pp", ("cp", "tp"), None)
    return jax.shard_map(shards, mesh=mesh, in_specs=in_specs, out_specs=out_specs, check_vma=False)
```

```python
import functools
import math

import jax
import jax.numpy as jnp
from jax import lax
from jax.experimental import pallas as pl
from jax.experimental.pallas import tpu as pltpu
from jax.sharding import PartitionSpec as P

HD = 128
SPAN = 128
LOG_SCALE = math.log2(math.e) / math.sqrt(HD)
MESH = pl.DeviceIdType.MESH


def kernel(
    n, tps, pps, kv_heads, group,
    order_ref, q_ref, k_ref, v_ref, out_ref,
    qbuf, kvbuf, obuf, bias, score_a, score_b, part_mixed, part_top, part_total,
    qsem, lsem, right_send, right_recv, left_send, left_recv, out_send, out_recv,
):
    rows = q_ref.shape[0]
    me = lax.axis_index("cp")
    my_tp = lax.axis_index("tp")
    my_pp = lax.axis_index("pp")
    next_pp = lax.rem(my_pp + 1, pps)
    last_pp = lax.rem(my_pp + pps - 1, pps)
    part = rows // tps
    width = group * HD
    pieces = group // 2
    piece_width = 2 * HD

    own = []
    for h in range(kv_heads):
        for which, ref in enumerate((k_ref, v_ref)):
            copy = pltpu.make_async_copy(
                ref.at[:, pl.ds(h * HD, HD)], kvbuf.at[h, me, which], lsem.at[h, which]
            )
            copy.start()
            own.append(copy)
    q_copies = []
    for h in range(kv_heads):
        copy = pltpu.make_async_copy(
            q_ref.at[:, pl.ds(h * width, width)], qbuf.at[:, pl.ds(h * width, width)], qsem.at[h]
        )
        copy.start()
        q_copies.append(copy)

    barrier = pltpu.get_barrier_semaphore()

    @pl.when(me > 0)
    def _():
        pl.semaphore_signal(barrier, inc=1, device_id={"cp": me - 1}, device_id_type=MESH)

    @pl.when(me < n - 1)
    def _():
        pl.semaphore_signal(barrier, inc=1, device_id={"cp": me + 1}, device_id_type=MESH)

    for t in range(tps):
        for other in (next_pp, last_pp):
            pl.semaphore_signal(
                barrier, inc=1, device_id={"pp": other, "tp": t}, device_id_type=MESH
            )
    near = jnp.where(me > 0, 1, 0) + jnp.where(me < n - 1, 1, 0)
    pl.semaphore_wait(barrier, 2 * tps + near)

    def to_right(h, k):
        slot = me - k
        return pltpu.make_async_remote_copy(
            src_ref=kvbuf.at[h, slot], dst_ref=kvbuf.at[h, slot],
            send_sem=right_send.at[h, k], recv_sem=right_recv.at[h, k],
            device_id={"cp": me + 1}, device_id_type=MESH,
        )

    def to_left(h, k):
        slot = me + k
        return pltpu.make_async_remote_copy(
            src_ref=kvbuf.at[h, slot], dst_ref=kvbuf.at[h, slot],
            send_sem=left_send.at[h, k], recv_sem=left_recv.at[h, k],
            device_id={"cp": me - 1}, device_id_type=MESH,
        )

    def from_left(h, k):
        return pltpu.make_async_remote_copy(
            src_ref=kvbuf.at[h, me - k], dst_ref=kvbuf.at[h, me - k],
            send_sem=right_send.at[h, k - 1], recv_sem=right_recv.at[h, k - 1],
            device_id={"cp": me - 1}, device_id_type=MESH,
        )

    def from_right(h, k):
        return pltpu.make_async_remote_copy(
            src_ref=kvbuf.at[h, me + k], dst_ref=kvbuf.at[h, me + k],
            send_sem=left_send.at[h, k - 1], recv_sem=left_recv.at[h, k - 1],
            device_id={"cp": me + 1}, device_id_type=MESH,
        )

    def send_own(h, inward):
        if not inward:
            own[2 * h].wait()
            own[2 * h + 1].wait()
        right_half = me >= n // 2

        @pl.when((me < n - 1) & (jnp.logical_not(right_half) if inward else right_half))
        def _():
            to_right(h, 0).start()

        @pl.when((me > 0) & (right_half if inward else jnp.logical_not(right_half)))
        def _():
            to_left(h, 0).start()

    def take(h, k):
        @pl.when(me - k >= 0)
        def _():
            from_left(h, k).wait_recv()

            @pl.when(me < n - 1)
            def _():
                to_right(h, k).start()

        @pl.when(me + k <= n - 1)
        def _():
            from_right(h, k).wait_recv()

            @pl.when(me > 0)
            def _():
                to_left(h, k).start()

    def out_copy(h, piece, t):
        first = pl.multiple_of(h * width + piece * piece_width, HD)
        index = (h * pieces + piece) * tps
        return pltpu.make_async_remote_copy(
            src_ref=obuf.at[pl.ds(t * part, part), pl.ds(first, piece_width)],
            dst_ref=out_ref.at[:, pl.ds(pl.multiple_of(my_tp * kv_heads * width + first, HD), piece_width)],
            send_sem=out_send.at[index + t], recv_sem=out_recv.at[index + my_tp],
            device_id={"pp": next_pp, "tp": t}, device_id_type=MESH,
        )

    def out_arrival(h, piece, t):
        first = pl.multiple_of(h * width + piece * piece_width, HD)
        index = (h * pieces + piece) * tps
        return pltpu.make_async_remote_copy(
            src_ref=obuf.at[pl.ds(0, part), pl.ds(first, piece_width)],
            dst_ref=out_ref.at[:, pl.ds(t * kv_heads * width + first, piece_width)],
            send_sem=out_send.at[index + t], recv_sem=out_recv.at[index + t],
            device_id={"pp": last_pp, "tp": t}, device_id_type=MESH,
        )

    send_own(0, False)
    send_own(0, True)
    if kv_heads > 1:
        send_own(1, False)

    spans = rows // SPAN
    row_in = lax.broadcasted_iota(jnp.int32, (SPAN, SPAN), 0)
    col_in = lax.broadcasted_iota(jnp.int32, (SPAN, SPAN), 1)
    for i in range(spans):
        query_span = order_ref[me * spans + i]

        def mask_span(j, _):
            gap = (query_span - order_ref[j]) * SPAN
            seen = col_in - row_in <= gap
            bias[j, pl.ds(i * SPAN, SPAN), :] = jnp.where(seen, 0.0, -1e30).astype(jnp.float32)
            return 0

        lax.fori_loop(0, n * spans, mask_span, 0)

    near_count = n - 2
    left_half = me < n // 2
    near_slot = jnp.where(left_half, 0, 2)
    late_slot = jnp.where(left_half, n - 2, 1)
    last_slot = jnp.where(left_half, n - 1, 0)
    inner = (me > 0) & (me < n - 1)

    def block(h, slot, count, which):
        return kvbuf[h, pl.ds(slot, count), which].reshape(count * rows, HD)

    def head_columns(h, g):
        return pl.ds(pl.multiple_of(h * width + g * HD, HD), HD)

    def score_of(h, g, slot, count):
        return lax.dot_general(
            qbuf[:, head_columns(h, g)], block(h, slot, count, 0),
            (((1,), (1,)), ((), ())), preferred_element_type=jnp.float32,
        )

    def masked(score, slot, count):
        masks = [bias[slot * spans + j] for j in range(count * spans)]
        return score + jnp.concatenate(masks, axis=1)

    def weigh(h, score, top, slot, count):
        weight = jnp.exp2((score - top) * LOG_SCALE)
        total = jnp.sum(weight, axis=1, keepdims=True)
        mixed = jnp.dot(
            weight.astype(jnp.bfloat16), block(h, slot, count, 1),
            preferred_element_type=jnp.float32,
        )
        return mixed, total

    def finish(h, g, mixed, total):
        obuf[:, head_columns(h, g)] = (mixed / total).astype(jnp.bfloat16)

    def send_piece(h, piece):
        for t in range(tps):
            out_copy(h, piece, t).start()

    def pairs(h, slot, count, done, between):
        score_a[:, : count * rows] = score_of(h, 0, slot, count)

        def pair(i, _):
            score_b[:, : count * rows] = score_of(h, 2 * i + 1, slot, count)
            done(2 * i, masked(score_a[:, : count * rows], slot, count))
            following = jnp.minimum(2 * i + 2, group - 1)
            score_a[:, : count * rows] = score_of(h, following, slot, count)
            done(2 * i + 1, masked(score_b[:, : count * rows], slot, count))
            between(i)
            return 0

        lax.fori_loop(0, group // 2, pair, 0)

    taken = set()

    def need(h, furthest):
        for k in range(1, furthest + 1):
            if ("inner", h, k) not in taken:
                take(h, k)
            elif ("ends", h, k) not in taken:
                @pl.when(jnp.logical_not(inner))
                def _():
                    take(h, k)
            taken.update({("inner", h, k), ("ends", h, k)})

    def relays(h, furthest, step):
        wanted = [k for k in range(1, furthest + 1) if ("inner", h, k) not in taken]
        taken.update(("inner", h, k) for k in wanted)
        return [(h, k, step) for k in wanted]

    def pass_on(i, steps):
        for h, k, step in steps:
            @pl.when((i == step) & inner)
            def _():
                take(h, k)

    def whole_head(h, steps):
        def done(g, score):
            top = jnp.max(score, axis=1, keepdims=True)
            finish(h, g, *weigh(h, score, top, 0, n))

        def between(i):
            send_piece(h, i)
            pass_on(i, steps)

        pairs(h, 0, n, done, between)

    def first_part(h, state, slot, count, steps):
        def done(g, score):
            top = jnp.max(score, axis=1, keepdims=True)
            mixed, total = weigh(h, score, top, slot, count)
            part_mixed[state, g] = mixed
            part_top[state, g] = jnp.broadcast_to(top, (rows, HD))
            part_total[state, g] = jnp.broadcast_to(total, (rows, HD))

        pairs(h, slot, count, done, lambda i: pass_on(i, steps))

    def add_slot(h, state, slot, final):
        def pair(i, _):
            for g in (2 * i, 2 * i + 1):
                score = masked(score_of(h, g, slot, 1), slot, 1)
                before = part_top[state, g]
                top = jnp.maximum(before, jnp.max(score, axis=1, keepdims=True))
                fade = jnp.exp2((before - top) * LOG_SCALE)
                mixed, total = weigh(h, score, top[:, :1], slot, 1)
                mixed = part_mixed[state, g] * fade + mixed
                total = part_total[state, g] * fade + total
                if final:
                    finish(h, g, mixed, total)
                else:
                    part_mixed[state, g] = mixed
                    part_top[state, g] = top
                    part_total[state, g] = total
            if final:
                send_piece(h, i)
            return 0

        lax.fori_loop(0, group // 2, pair, 0)

    last = kv_heads - 1
    own_sent = 2
    need(0, 1)
    if kv_heads > 1:
        send_own(1, True)
    for h in range(max(kv_heads - 2, 0)):
        need(h, 1)
        if own_sent < kv_heads:
            send_own(own_sent, False)
            send_own(own_sent, True)
            own_sent += 1
        need(h, n - 1)
        q_copies[h].wait()
        steps = relays(h + 1, n - 2, 0)
        if h == kv_heads - 3:
            steps += relays(last, 1, 2)
        whole_head(h, steps)
    need(last, n - 3)
    q_copies[last].wait()
    first_part(last, 1, near_slot, near_count, relays(last, n - 2, 2))
    if kv_heads > 1:
        wide = jnp.where(left_half, 0, 1)
        need(last - 1, n - 2)
        q_copies[last - 1].wait()
        first_part(last - 1, 0, wide, n - 1, [])
        need(last - 1, n - 1)
        add_slot(last - 1, 0, last_slot, True)
    need(last, n - 2)
    add_slot(last, 1, late_slot, False)
    need(last, n - 1)
    add_slot(last, 1, last_slot, True)

    for h in range(kv_heads):
        for k in range(n - 1):
            @pl.when((me - k >= 0) & (me < n - 1))
            def _():
                to_right(h, k).wait_send()

            @pl.when((me + k <= n - 1) & (me > 0))
            def _():
                to_left(h, k).wait_send()

    for h in range(kv_heads):
        def drain(piece, _):
            for t in range(tps):
                out_copy(h, piece, t).wait_send()
                out_arrival(h, piece, t).wait_recv()
            return 0

        lax.fori_loop(0, pieces, drain, 0)


def shards(queries, keys, values, span_order):
    query_rows, key_local, value_local = queries[0], keys[0], values[0]
    rows = query_rows.shape[0]
    kv_heads = key_local.shape[1] // HD
    group = query_rows.shape[1] // HD // kv_heads
    n, tps, pps = lax.axis_size("cp"), lax.axis_size("tp"), lax.axis_size("pp")
    copies = kv_heads * (group // 2) * tps
    dma = pltpu.SemaphoreType.DMA
    result = pl.pallas_call(
        functools.partial(kernel, n, tps, pps, kv_heads, group),
        out_shape=pltpu.VMEM((rows // tps, tps * query_rows.shape[1]), jnp.bfloat16),
        in_specs=[
            pl.BlockSpec(memory_space=pltpu.SMEM),
            pl.BlockSpec(memory_space=pl.ANY),
            pl.BlockSpec(memory_space=pl.ANY),
            pl.BlockSpec(memory_space=pl.ANY),
        ],
        out_specs=pl.BlockSpec(memory_space=pltpu.VMEM),
        scratch_shapes=[
            pltpu.VMEM(query_rows.shape, jnp.bfloat16),
            pltpu.VMEM((kv_heads, n, 2, rows, HD), jnp.bfloat16),
            pltpu.VMEM(query_rows.shape, jnp.bfloat16),
            pltpu.VMEM((n * rows // SPAN, rows, SPAN), jnp.float32),
            pltpu.VMEM((rows, n * rows), jnp.float32),
            pltpu.VMEM((rows, n * rows), jnp.float32),
            pltpu.VMEM((2, group, rows, HD), jnp.float32),
            pltpu.VMEM((2, group, rows, HD), jnp.float32),
            pltpu.VMEM((2, group, rows, HD), jnp.float32),
            dma((kv_heads,)),
            dma((kv_heads, 2)),
            dma((kv_heads, n)),
            dma((kv_heads, n)),
            dma((kv_heads, n)),
            dma((kv_heads, n)),
            dma((copies,)),
            dma((copies,)),
        ],
        compiler_params=pltpu.CompilerParams(
            collective_id=0, has_side_effects=True, vmem_limit_bytes=56 * 1024 * 1024
        ),
    )(span_order, query_rows, key_local, value_local)
    return result[None]


def solution(mesh):
    in_specs = (P("pp", "cp", "tp"), P("pp", "cp", "tp"), P("pp", "cp", "tp"), P())
    out_specs = P("pp", ("cp", "tp"), None)
    return jax.shard_map(shards, mesh=mesh, in_specs=in_specs, out_specs=out_specs, check_vma=False)
```

```python
import functools
import math

import jax
import jax.numpy as jnp
from jax import lax
from jax.experimental import pallas as pl
from jax.experimental.pallas import tpu as pltpu
from jax.sharding import PartitionSpec as P

HD = 128
SPAN = 128
LOG_SCALE = math.log2(math.e) / math.sqrt(HD)
MESH = pl.DeviceIdType.MESH


def kernel(
    n, tps, pps, kv_heads, group,
    order_ref, q_ref, k_ref, v_ref, out_ref,
    qbuf, kvbuf, obuf, bias, score_a, score_b, part_mixed, part_top, part_total,
    qsem, lsem, right_send, right_recv, left_send, left_recv, out_send, out_recv,
):
    rows = q_ref.shape[0]
    me = lax.axis_index("cp")
    my_tp = lax.axis_index("tp")
    my_pp = lax.axis_index("pp")
    next_pp = lax.rem(my_pp + 1, pps)
    last_pp = lax.rem(my_pp + pps - 1, pps)
    part = rows // tps
    width = group * HD
    pieces = group // 2
    piece_width = 2 * HD

    own = []
    for h in range(kv_heads):
        for which, ref in enumerate((k_ref, v_ref)):
            copy = pltpu.make_async_copy(
                ref.at[:, pl.ds(h * HD, HD)], kvbuf.at[h, me, which], lsem.at[h, which]
            )
            copy.start()
            own.append(copy)
    q_copies = []
    for h in range(kv_heads):
        copy = pltpu.make_async_copy(
            q_ref.at[:, pl.ds(h * width, width)], qbuf.at[:, pl.ds(h * width, width)], qsem.at[h]
        )
        copy.start()
        q_copies.append(copy)

    barrier = pltpu.get_barrier_semaphore()

    @pl.when(me > 0)
    def _():
        pl.semaphore_signal(barrier, inc=1, device_id={"cp": me - 1}, device_id_type=MESH)

    @pl.when(me < n - 1)
    def _():
        pl.semaphore_signal(barrier, inc=1, device_id={"cp": me + 1}, device_id_type=MESH)

    for t in range(tps):
        for other in (next_pp, last_pp):
            pl.semaphore_signal(
                barrier, inc=1, device_id={"pp": other, "tp": t}, device_id_type=MESH
            )
    near = jnp.where(me > 0, 1, 0) + jnp.where(me < n - 1, 1, 0)
    pl.semaphore_wait(barrier, 2 * tps + near)

    def to_right(h, k):
        slot = me - k
        return pltpu.make_async_remote_copy(
            src_ref=kvbuf.at[h, slot], dst_ref=kvbuf.at[h, slot],
            send_sem=right_send.at[h, k], recv_sem=right_recv.at[h, k],
            device_id={"cp": me + 1}, device_id_type=MESH,
        )

    def to_left(h, k):
        slot = me + k
        return pltpu.make_async_remote_copy(
            src_ref=kvbuf.at[h, slot], dst_ref=kvbuf.at[h, slot],
            send_sem=left_send.at[h, k], recv_sem=left_recv.at[h, k],
            device_id={"cp": me - 1}, device_id_type=MESH,
        )

    def from_left(h, k):
        return pltpu.make_async_remote_copy(
            src_ref=kvbuf.at[h, me - k], dst_ref=kvbuf.at[h, me - k],
            send_sem=right_send.at[h, k - 1], recv_sem=right_recv.at[h, k - 1],
            device_id={"cp": me - 1}, device_id_type=MESH,
        )

    def from_right(h, k):
        return pltpu.make_async_remote_copy(
            src_ref=kvbuf.at[h, me + k], dst_ref=kvbuf.at[h, me + k],
            send_sem=left_send.at[h, k - 1], recv_sem=left_recv.at[h, k - 1],
            device_id={"cp": me + 1}, device_id_type=MESH,
        )

    def send_own(h, inward):
        if not inward:
            own[2 * h].wait()
            own[2 * h + 1].wait()
        right_half = me >= n // 2

        @pl.when((me < n - 1) & (jnp.logical_not(right_half) if inward else right_half))
        def _():
            to_right(h, 0).start()

        @pl.when((me > 0) & (right_half if inward else jnp.logical_not(right_half)))
        def _():
            to_left(h, 0).start()

    def take(h, k):
        @pl.when(me - k >= 0)
        def _():
            from_left(h, k).wait_recv()

            @pl.when(me < n - 1)
            def _():
                to_right(h, k).start()

        @pl.when(me + k <= n - 1)
        def _():
            from_right(h, k).wait_recv()

            @pl.when(me > 0)
            def _():
                to_left(h, k).start()

    def out_copy(h, piece, t):
        first = pl.multiple_of(h * width + piece * piece_width, HD)
        index = (h * pieces + piece) * tps
        return pltpu.make_async_remote_copy(
            src_ref=obuf.at[pl.ds(t * part, part), pl.ds(first, piece_width)],
            dst_ref=out_ref.at[:, pl.ds(pl.multiple_of(my_tp * kv_heads * width + first, HD), piece_width)],
            send_sem=out_send.at[index + t], recv_sem=out_recv.at[index + my_tp],
            device_id={"pp": next_pp, "tp": t}, device_id_type=MESH,
        )

    def out_arrival(h, piece, t):
        first = pl.multiple_of(h * width + piece * piece_width, HD)
        index = (h * pieces + piece) * tps
        return pltpu.make_async_remote_copy(
            src_ref=obuf.at[pl.ds(0, part), pl.ds(first, piece_width)],
            dst_ref=out_ref.at[:, pl.ds(t * kv_heads * width + first, piece_width)],
            send_sem=out_send.at[index + t], recv_sem=out_recv.at[index + t],
            device_id={"pp": last_pp, "tp": t}, device_id_type=MESH,
        )

    send_own(0, False)
    send_own(0, True)
    if kv_heads > 1:
        send_own(1, False)

    spans = rows // SPAN
    row_in = lax.broadcasted_iota(jnp.int32, (SPAN, SPAN), 0)
    col_in = lax.broadcasted_iota(jnp.int32, (SPAN, SPAN), 1)
    for i in range(spans):
        query_span = order_ref[me * spans + i]

        def mask_span(j, _):
            gap = (query_span - order_ref[j]) * SPAN
            seen = col_in - row_in <= gap
            bias[j, pl.ds(i * SPAN, SPAN), :] = jnp.where(seen, 0.0, -1e30).astype(jnp.float32)
            return 0

        lax.fori_loop(0, n * spans, mask_span, 0)

    near_count = n - 2
    left_half = me < n // 2
    near_slot = jnp.where(left_half, 0, 2)
    late_slot = jnp.where(left_half, n - 2, 0)
    inner = (me > 0) & (me < n - 1)

    def block(h, slot, count, which):
        return kvbuf[h, pl.ds(slot, count), which].reshape(count * rows, HD)

    def head_columns(h, g):
        return pl.ds(pl.multiple_of(h * width + g * HD, HD), HD)

    def score_of(h, g, slot, count):
        return lax.dot_general(
            qbuf[:, head_columns(h, g)], block(h, slot, count, 0),
            (((1,), (1,)), ((), ())), preferred_element_type=jnp.float32,
        )

    def masked(score, slot, count):
        masks = [bias[slot * spans + j] for j in range(count * spans)]
        return score + jnp.concatenate(masks, axis=1)

    def weigh(h, score, top, slot, count):
        weight = jnp.exp2((score - top) * LOG_SCALE)
        total = jnp.sum(weight, axis=1, keepdims=True)
        mixed = jnp.dot(
            weight.astype(jnp.bfloat16), block(h, slot, count, 1),
            preferred_element_type=jnp.float32,
        )
        return mixed, total

    def finish(h, g, mixed, total):
        obuf[:, head_columns(h, g)] = (mixed / total).astype(jnp.bfloat16)

    def send_piece(h, piece):
        for t in range(tps):
            out_copy(h, piece, t).start()

    def pairs(h, slot, count, done, between):
        score_a[:, : count * rows] = score_of(h, 0, slot, count)

        def pair(i, _):
            score_b[:, : count * rows] = score_of(h, 2 * i + 1, slot, count)
            done(2 * i, masked(score_a[:, : count * rows], slot, count))
            following = jnp.minimum(2 * i + 2, group - 1)
            score_a[:, : count * rows] = score_of(h, following, slot, count)
            done(2 * i + 1, masked(score_b[:, : count * rows], slot, count))
            between(i)
            return 0

        lax.fori_loop(0, group // 2, pair, 0)

    taken = set()

    def need(h, furthest):
        for k in range(1, furthest + 1):
            if ("inner", h, k) not in taken:
                take(h, k)
            elif ("ends", h, k) not in taken:
                @pl.when(jnp.logical_not(inner))
                def _():
                    take(h, k)
            taken.update({("inner", h, k), ("ends", h, k)})

    def relays(h, furthest, step):
        wanted = [k for k in range(1, furthest + 1) if ("inner", h, k) not in taken]
        taken.update(("inner", h, k) for k in wanted)
        return [(h, k, min(step + 2 * (k - 1), group // 2 - 1)) for k in wanted]

    def pass_on(i, steps):
        for h, k, step in steps:
            @pl.when((i == step) & inner)
            def _():
                take(h, k)

    def whole_head(h, steps):
        def done(g, score):
            top = jnp.max(score, axis=1, keepdims=True)
            finish(h, g, *weigh(h, score, top, 0, n))

        def between(i):
            send_piece(h, i)
            pass_on(i, steps)

        pairs(h, 0, n, done, between)

    def first_part(h, slot, count, steps):
        def done(g, score):
            top = jnp.max(score, axis=1, keepdims=True)
            mixed, total = weigh(h, score, top, slot, count)
            part_mixed[g] = mixed
            part_top[g] = jnp.broadcast_to(top, (rows, HD))
            part_total[g] = jnp.broadcast_to(total, (rows, HD))

        pairs(h, slot, count, done, lambda i: pass_on(i, steps))

    def last_part(h, slot, count):
        together = 4

        def some(i, _):
            for step in range(together):
                g = together * i + step
                score = masked(score_of(h, g, slot, count), slot, count)
                before = part_top[g]
                top = jnp.maximum(before, jnp.max(score, axis=1, keepdims=True))
                fade = jnp.exp2((before - top) * LOG_SCALE)
                mixed, total = weigh(h, score, top[:, :1], slot, count)
                finish(h, g, part_mixed[g] * fade + mixed, part_total[g] * fade + total)
                if step % 2 == 1:
                    send_piece(h, (together * i + step) // 2)
            return 0

        lax.fori_loop(0, group // together, some, 0)

    last = kv_heads - 1
    own_sent = 2
    need(0, 1)
    if kv_heads > 1:
        send_own(1, True)
    for h in range(max(kv_heads - 2, 0)):
        need(h, 1)
        if own_sent < kv_heads:
            send_own(own_sent, False)
            send_own(own_sent, True)
            own_sent += 1
        need(h, n - 1)
        q_copies[h].wait()
        steps = relays(h + 1, n - 2, 0)
        if h == kv_heads - 3:
            steps += relays(last, 1, 3)
        whole_head(h, steps)
    need(last, n - 3)
    q_copies[last].wait()
    first_part(last, near_slot, near_count, relays(last, n - 2, 0))
    if kv_heads > 1:
        need(last - 1, n - 1)
        q_copies[last - 1].wait()
        whole_head(last - 1, [])
    need(last, n - 1)
    last_part(last, late_slot, 2)

    for h in range(kv_heads):
        for k in range(n - 1):
            @pl.when((me - k >= 0) & (me < n - 1))
            def _():
                to_right(h, k).wait_send()

            @pl.when((me + k <= n - 1) & (me > 0))
            def _():
                to_left(h, k).wait_send()

    for h in range(kv_heads):
        def drain(piece, _):
            for t in range(tps):
                out_copy(h, piece, t).wait_send()
                out_arrival(h, piece, t).wait_recv()
            return 0

        lax.fori_loop(0, pieces, drain, 0)


def shards(queries, keys, values, span_order):
    query_rows, key_local, value_local = queries[0], keys[0], values[0]
    rows = query_rows.shape[0]
    kv_heads = key_local.shape[1] // HD
    group = query_rows.shape[1] // HD // kv_heads
    n, tps, pps = lax.axis_size("cp"), lax.axis_size("tp"), lax.axis_size("pp")
    copies = kv_heads * (group // 2) * tps
    dma = pltpu.SemaphoreType.DMA
    result = pl.pallas_call(
        functools.partial(kernel, n, tps, pps, kv_heads, group),
        out_shape=pltpu.VMEM((rows // tps, tps * query_rows.shape[1]), jnp.bfloat16),
        in_specs=[
            pl.BlockSpec(memory_space=pltpu.SMEM),
            pl.BlockSpec(memory_space=pl.ANY),
            pl.BlockSpec(memory_space=pl.ANY),
            pl.BlockSpec(memory_space=pl.ANY),
        ],
        out_specs=pl.BlockSpec(memory_space=pltpu.VMEM),
        scratch_shapes=[
            pltpu.VMEM(query_rows.shape, jnp.bfloat16),
            pltpu.VMEM((kv_heads, n, 2, rows, HD), jnp.bfloat16),
            pltpu.VMEM(query_rows.shape, jnp.bfloat16),
            pltpu.VMEM((n * rows // SPAN, rows, SPAN), jnp.float32),
            pltpu.VMEM((rows, n * rows), jnp.float32),
            pltpu.VMEM((rows, n * rows), jnp.float32),
            pltpu.VMEM((group, rows, HD), jnp.float32),
            pltpu.VMEM((group, rows, HD), jnp.float32),
            pltpu.VMEM((group, rows, HD), jnp.float32),
            dma((kv_heads,)),
            dma((kv_heads, 2)),
            dma((kv_heads, n)),
            dma((kv_heads, n)),
            dma((kv_heads, n)),
            dma((kv_heads, n)),
            dma((copies,)),
            dma((copies,)),
        ],
        compiler_params=pltpu.CompilerParams(
            collective_id=0, has_side_effects=True, vmem_limit_bytes=56 * 1024 * 1024
        ),
    )(span_order, query_rows, key_local, value_local)
    return result[None]


def solution(mesh):
    in_specs = (P("pp", "cp", "tp"), P("pp", "cp", "tp"), P("pp", "cp", "tp"), P())
    out_specs = P("pp", ("cp", "tp"), None)
    return jax.shard_map(shards, mesh=mesh, in_specs=in_specs, out_specs=out_specs, check_vma=False)
```
